256 devices in a mesh: seq: 128 (over x, z, y_lo, core), head: 2 (over y_hi).
Axes of the slice: x: 4, y: 4 (y_hi: 2, y_lo: 2; y = y_hi * 2 + y_lo), z: 8, core: 2. Of those that a mesh axis runs over, the one named last changes fastest.
Arguments:
- queries: bfloat16 [1, 32768, 16, 128], P(None, 'seq', 'head'), may hold values from -6 to 6
- keys: bfloat16 [1, 32768, 4, 128], P(None, 'seq', 'head'), may hold values from -6 to 6
- values: bfloat16 [1, 32768, 4, 128], P(None, 'seq', 'head'), may hold values from -6 to 6
- norm_gain: float32 [16, 128], P('head'), may hold values from 0.25 to 1.75
- out_grad: bfloat16 [1, 32768, 16, 128], P(None, 'seq', 'head'), may hold values from -6 to 6
- window_reach: int32 [1, 128], P(None, 'seq'), may hold values from 0 to 256
- partner_mask: int32 [1, 128, 6], P(None, 'seq'), may hold values 0 or 1
Outputs:
- normed: bfloat16 [1, 32768, 16, 128], P(None, 'seq', 'head')
- query_grad: bfloat16 [1, 32768, 16, 128], P(None, 'seq', 'head')
- key_gradient: bfloat16 [1, 32768, 4, 128], P(None, 'seq', 'head')
- value_gradient: bfloat16 [1, 32768, 4, 128], P(None, 'seq', 'head')
The draws below stay inside these ranges and needn't reach their ends.
All inputs are finite; a program needn't handle non-finite values. No bound on the sum of `partner_mask` on one device may be relied on, other than what follows from the above.
Results may differ from the reference program's by a relative error of at most 0.029.
Values may be sent and summed in bfloat16 or wider, within the bound.
No kernel may reach another device: no remote copies, remote signals or barrier semaphores. Data moves between devices by JAX's collectives and lax.ppermute only.
A program may use at most 64 MiB of HBM per device.

```python
import math
import jax
import jax.numpy as jnp
from jax import lax

QUERY_HEADS = 16
KEY_VALUE_HEADS = 4
HEAD_DIMENSION = 128
BLOCK_TOKENS = 256
SEQUENCE_COUNT = 1
BLOCK_COUNT = 128
SEQUENCE_TOKENS = 32768
QUERIES_PER_KEY = 4
NLEVEL = 6


def draw_queries(key, part):
    noise_random_seed = jax.random.fold_in(key, 5)
    sampled_numbers = jnp.clip(jax.random.normal(noise_random_seed, (SEQUENCE_COUNT, SEQUENCE_TOKENS, QUERY_HEADS, HEAD_DIMENSION), jnp.float32), -6.0, 6.0)
    return sampled_numbers.astype(jnp.bfloat16)


def draw_keys(key, part):
    noise_random_seed = jax.random.fold_in(key, 6)
    sampled_numbers = jnp.clip(jax.random.normal(noise_random_seed, (SEQUENCE_COUNT, SEQUENCE_TOKENS, KEY_VALUE_HEADS, HEAD_DIMENSION), jnp.float32), -6.0, 6.0)
    return sampled_numbers.astype(jnp.bfloat16)


def draw_values(key, part):
    child_seeds = jax.random.split(jax.random.fold_in(key, 7), 3)
    small_noise = jnp.exp(jax.random.uniform(child_seeds[0], (KEY_VALUE_HEADS,), jnp.float32, -0.15, 0.15))
    head_multiplier = 3.0 ** (0.5 * jnp.arange(KEY_VALUE_HEADS, dtype=jnp.float32) / (KEY_VALUE_HEADS - 1)) * small_noise
    row_scale = jnp.exp(jax.random.uniform(child_seeds[1], (SEQUENCE_COUNT, SEQUENCE_TOKENS, 1, 1), jnp.float32, 0.0, 1.1))
    starting_sample = jax.random.normal(child_seeds[2], (SEQUENCE_COUNT, SEQUENCE_TOKENS, KEY_VALUE_HEADS, HEAD_DIMENSION), jnp.float32)
    sampled_numbers = jnp.clip(starting_sample * row_scale * head_multiplier[None, None, :, None], -6.0, 6.0)
    return sampled_numbers.astype(jnp.bfloat16)


def plant(values, own_key, smallest, high):
    place = [jax.random.randint(jax.random.fold_in(own_key, axis), (), 0, length) for axis, length in enumerate(values.shape)]
    main_axis = values.shape.index(max(values.shape))
    beside = place[:main_axis] + [(place[main_axis] + 1) % values.shape[main_axis]] + place[main_axis + 1:]
    return values.at[tuple(place)].set(smallest).at[tuple(beside)].set(high)


def steps_of(rng, dims, pieces, low, top_value):
    loudness = 1.0
    for axis_at, blocks in pieces:
        heights = jax.random.uniform(jax.random.fold_in(jax.random.fold_in(rng, 6), axis_at), (blocks,), jnp.float32, low / len(pieces), top_value / len(pieces))
        loudness = loudness * jnp.repeat(jnp.exp(heights), dims[axis_at] // blocks).reshape((-1,) + (1,) * (len(dims) - 1 - axis_at))
    return loudness


def centred(key, dims, deviation, bound, cuts=(), kind=jnp.bfloat16):
    drawn = jax.random.normal(key, dims, jnp.float32) * deviation
    if len(cuts) > 0:
        drawn = steps_of(key, dims, cuts, -0.22, 0.18) * drawn
    return jnp.clip(drawn, min=-bound, max=bound).astype(kind)


def setup_inputs(seed: int = 0) -> dict:
    key_list = jax.random.split(jax.random.key(seed), 8)
    queries = draw_queries(jax.random.fold_in(key_list[7], 71), 0)
    keys = draw_keys(jax.random.fold_in(key_list[7], 71), 0)
    values = draw_values(jax.random.fold_in(key_list[7], 71), 0)
    norm_gain = jnp.clip(1.0 + 0.15 * jax.random.normal(key_list[3], (QUERY_HEADS, HEAD_DIMENSION), jnp.float32), 0.25, 1.75)
    out_grad = centred(key_list[4], (SEQUENCE_COUNT, SEQUENCE_TOKENS, QUERY_HEADS, HEAD_DIMENSION), 1.0, 6.0, ((1, 128), (2, 2)))
    window_reach = plant(jax.random.randint(key_list[5], (SEQUENCE_COUNT, BLOCK_COUNT), 0, BLOCK_TOKENS + 1), jax.random.fold_in(key_list[5], 1), 0, BLOCK_TOKENS).astype(jnp.int32)
    partner_mask = plant((jax.random.randint(key_list[6], (SEQUENCE_COUNT, BLOCK_COUNT, NLEVEL), 0, 4) < 3).astype(jnp.int32), jax.random.fold_in(key_list[6], 1), 0, 1)
    return dict(queries=queries, keys=keys, values=values, norm_gain=norm_gain, out_grad=out_grad, window_reach=window_reach, partner_mask=partner_mask)


epsilon = 1e-06

def rounded(tensor):
    return lax.optimization_barrier(tensor.astype(jnp.bfloat16)).astype(jnp.float32)

def reference(queries, keys, values, norm_gain, out_grad, window_reach, partner_mask):
    score_scale = 1.0 / math.sqrt(HEAD_DIMENSION)
    offsets = jnp.array([0, 1] + [2 ** level for level in range(1, NLEVEL + 1)], jnp.int32)
    positions = jnp.arange(BLOCK_TOKENS, dtype=jnp.int32)
    blocked_queries = queries.reshape(SEQUENCE_COUNT * BLOCK_COUNT, BLOCK_TOKENS, KEY_VALUE_HEADS, QUERIES_PER_KEY, HEAD_DIMENSION).astype(jnp.float32)
    blocked_keys = keys.reshape(SEQUENCE_COUNT * BLOCK_COUNT, BLOCK_TOKENS, KEY_VALUE_HEADS, HEAD_DIMENSION).astype(jnp.float32)
    blocked_values = values.reshape(SEQUENCE_COUNT * BLOCK_COUNT, BLOCK_TOKENS, KEY_VALUE_HEADS, HEAD_DIMENSION).astype(jnp.float32)

    def pattern(index):
        sequence = index // BLOCK_COUNT
        block_index = index % BLOCK_COUNT
        targets = block_index - offsets
        gathered = (sequence * BLOCK_COUNT + jnp.maximum(targets, 0)).astype(jnp.int32)
        own_mask = positions[None, :] <= positions[:, None]
        window = (positions[None, :] >= BLOCK_TOKENS - window_reach[sequence, block_index]) & (block_index >= 1)
        window = jnp.broadcast_to(window, (BLOCK_TOKENS, BLOCK_TOKENS))
        levels = (partner_mask[sequence, block_index] == 1) & (block_index >= offsets[2:])
        level_masks = jnp.broadcast_to(levels[:, None, None], (NLEVEL, BLOCK_TOKENS, BLOCK_TOKENS))
        allowed = jnp.concatenate([own_mask[None], window[None], level_masks], axis=0)
        return (gathered, allowed.transpose(1, 2, 0))

    def scores_of(index):
        gathered, allowed = pattern(index)
        raw_scores = jnp.einsum('uhgd,tshd->hgust', blocked_queries[index], blocked_keys[gathered]) * score_scale
        return (jnp.where(allowed[None, None], raw_scores, -jnp.inf), gathered)

    def forward(index):
        scores, gathered = scores_of(index)
        row_peak = lax.optimization_barrier(jnp.max(scores, axis=(3, 4)))
        log_total = row_peak + jnp.log(lax.optimization_barrier(jnp.sum(jnp.exp(scores - row_peak[..., None, None]), axis=(3, 4))))
        probabilities = rounded(jnp.exp(scores - log_total[..., None, None]))
        output = jnp.einsum('hgust,tshd->uhgd', probabilities, blocked_values[gathered])
        return (output.astype(jnp.bfloat16), log_total)
    block_ids = jnp.arange(SEQUENCE_COUNT * BLOCK_COUNT, dtype=jnp.int32)
    attn_blocks, log_totals = lax.map(forward, block_ids)
    attn_wide = lax.optimization_barrier(attn_blocks).astype(jnp.float32).reshape(SEQUENCE_COUNT, SEQUENCE_TOKENS, QUERY_HEADS, HEAD_DIMENSION)
    mean_square = lax.optimization_barrier(jnp.mean(attn_wide * attn_wide, axis=(2, 3)))
    inverse = 1.0 / jnp.sqrt(mean_square + epsilon)
    normed = (norm_gain * attn_wide * inverse[..., None, None]).astype(jnp.bfloat16)
    scaled_grad = norm_gain * out_grad.astype(jnp.float32)
    dot_total = lax.optimization_barrier(jnp.sum(scaled_grad * attn_wide, axis=(2, 3)))
    attention_gradient = rounded(scaled_grad * inverse[..., None, None] - attn_wide * (dot_total * inverse ** 3 / (QUERY_HEADS * HEAD_DIMENSION))[..., None, None])
    correction_rows = lax.optimization_barrier(jnp.sum(attention_gradient * attn_wide, axis=-1))
    gradient_blocks = attention_gradient.reshape(SEQUENCE_COUNT * BLOCK_COUNT, BLOCK_TOKENS, KEY_VALUE_HEADS, QUERIES_PER_KEY, HEAD_DIMENSION)
    correction_blocks = correction_rows.reshape(SEQUENCE_COUNT * BLOCK_COUNT, BLOCK_TOKENS, KEY_VALUE_HEADS, QUERIES_PER_KEY)

    def backward(carried, index):
        key_accumulator, value_accumulator = carried
        scores, gathered = scores_of(index)
        weights = jnp.exp(scores - log_totals[index][..., None, None])
        prob_grad = jnp.einsum('uhgd,tshd->hgust', gradient_blocks[index], blocked_values[gathered])
        score_grad = rounded(weights * (prob_grad - correction_blocks[index].transpose(1, 2, 0)[..., None, None]))
        query_part = jnp.einsum('hgust,tshd->uhgd', score_grad, blocked_keys[gathered]) * score_scale
        key_part = jnp.einsum('hgust,uhgd->tshd', score_grad, blocked_queries[index]) * score_scale
        value_part = jnp.einsum('hgust,uhgd->tshd', rounded(weights), gradient_blocks[index])
        return ((key_accumulator.at[gathered].add(key_part), value_accumulator.at[gathered].add(value_part)), query_part.astype(jnp.bfloat16))
    empty_gradients = jnp.zeros((SEQUENCE_COUNT * BLOCK_COUNT, BLOCK_TOKENS, KEY_VALUE_HEADS, HEAD_DIMENSION), jnp.float32)
    (key_accumulator, value_accumulator), query_parts = lax.scan(backward, (empty_gradients, empty_gradients), block_ids)
    query_grad = query_parts.reshape(SEQUENCE_COUNT, SEQUENCE_TOKENS, QUERY_HEADS, HEAD_DIMENSION)
    key_gradient = key_accumulator.astype(jnp.bfloat16).reshape(SEQUENCE_COUNT, SEQUENCE_TOKENS, KEY_VALUE_HEADS, HEAD_DIMENSION)
    value_gradient = value_accumulator.astype(jnp.bfloat16).reshape(SEQUENCE_COUNT, SEQUENCE_TOKENS, KEY_VALUE_HEADS, HEAD_DIMENSION)
    return (normed, query_grad, key_gradient, value_gradient)
```

```python
import functools
import math

import jax
import jax.numpy as jnp
from jax import lax
from jax.experimental import pallas as pl
from jax.experimental.pallas import tpu as pltpu
from jax.sharding import PartitionSpec as P


epsilon = 1e-06
NEG = -1e30
LOG2E = 1.4426950408889634
F32, BF16 = jnp.float32, jnp.bfloat16


def rotated(value, steps):
    count = lax.axis_size("seq")
    return lax.ppermute(value, "seq", [(s, (s + steps) % count) for s in range(count)])


def dot(a, b, ca, cb):
    return lax.dot_general(a, b, (((ca,), (cb,)), ((), ())), preferred_element_type=F32)


def masked(scores, thr, causal):
    rows = lax.broadcasted_iota(jnp.int32, scores.shape, 0)
    if causal:
        return jnp.where(rows <= lax.broadcasted_iota(jnp.int32, scores.shape, 1), scores, NEG)
    return jnp.where(rows >= thr, scores, NEG)


def forward_kernel(kinds, scale, first, last, thr_ref, q_ref, *refs):
    blocks = refs[: len(kinds)]
    refs = refs[len(kinds) :]
    heads = q_ref.shape[0]
    groups = blocks[0].shape[0] // 2
    per = heads // groups
    if first:
        og_ref, gain_ref, m_ref, l_ref, acc_ref, sg_ref = refs
        m_ref[...] = jnp.full_like(m_ref, NEG)
        l_ref[...] = jnp.zeros_like(l_ref)
        acc_ref[...] = jnp.zeros_like(acc_ref)
        for h in range(heads):
            sg_ref[h] = (og_ref[h].astype(F32) * gain_ref[h : h + 1, :]).T
    elif last:
        m_in, l_in, acc_in, sg_ref, attn_ref, log_ref, stats_ref, m_ref, l_ref, acc_ref = refs
        m_ref[...] = m_in[...]
        l_ref[...] = l_in[...]
        acc_ref[...] = acc_in[...]
    else:
        m_in, l_in, acc_in, m_ref, l_ref, acc_ref = refs
        m_ref[...] = m_in[...]
        l_ref[...] = l_in[...]
        acc_ref[...] = acc_in[...]
    for (slot, causal, uniform), block in zip(kinds, blocks):
        thr = thr_ref[slot]

        def step(block=block, thr=thr, causal=causal, uniform=uniform):
            for h in range(heads):
                g = h // per
                s = dot(block[g], q_ref[h], 1, 1) * (scale * LOG2E)
                if not uniform:
                    s = masked(s, thr, causal)
                old = m_ref[h : h + 1, :]
                new = jnp.maximum(old, jnp.max(s, axis=0, keepdims=True))
                p = jnp.exp2(s - new)
                alpha = jnp.exp2(old - new)
                m_ref[h : h + 1, :] = new
                l_ref[h : h + 1, :] = l_ref[h : h + 1, :] * alpha + jnp.sum(
                    p, axis=0, keepdims=True
                )
                acc_ref[h] = acc_ref[h] * alpha + dot(block[groups + g], p.astype(BF16), 0, 0)

        if uniform:
            pl.when(thr == 0)(step)
        else:
            step()
    if last:
        square = jnp.zeros((1, q_ref.shape[1]), F32)
        inner = jnp.zeros((1, q_ref.shape[1]), F32)
        for h in range(heads):
            total = l_ref[h : h + 1, :]
            log_ref[h : h + 1, :] = m_ref[h : h + 1, :] + jnp.log2(total)
            attn = (acc_ref[h] * (1.0 / total)).astype(BF16)
            attn_ref[h] = attn
            wide = attn.astype(F32)
            square = square + jnp.sum(wide * wide, axis=0, keepdims=True)
            inner = inner + jnp.sum(sg_ref[h] * wide, axis=0, keepdims=True)
        stats_ref[0:1, :] = square
        stats_ref[1:2, :] = inner


def gradient_kernel(features, mine_ref, other_ref, attn_ref, sg_ref, grad_ref, delta_ref):
    stats = mine_ref[...] + other_ref[...]
    inverse = lax.rsqrt(stats[0:1, :] / features + epsilon)
    back = stats[1:2, :] * (inverse * inverse * inverse) / features
    for h in range(attn_ref.shape[0]):
        wide = attn_ref[h].astype(F32)
        grad = (sg_ref[h] * inverse - wide * back).astype(BF16)
        delta_ref[h : h + 1, :] = jnp.sum(grad.astype(F32) * wide, axis=0, keepdims=True)
        grad_ref[h] = grad.T


def normed_kernel(features, mine_ref, other_ref, attn_ref, gain_ref, normed_ref):
    stats = mine_ref[0:1, :] + other_ref[0:1, :]
    inverse = lax.rsqrt(stats / features + epsilon)
    for h in range(attn_ref.shape[0]):
        wide = attn_ref[h].astype(F32) * inverse
        normed_ref[h] = (wide.T * gain_ref[h : h + 1, :]).astype(BF16)


def backward_kernel(kind, scale, first, thr_ref, q_ref, block, grad_ref, log_ref, delta_ref, *refs):
    slot, causal, uniform = kind
    heads = q_ref.shape[0]
    groups = block.shape[0] // 2
    per = heads // groups
    if first:
        out_ref, dq_ref = refs
    else:
        dq_in, out_ref, dq_ref = refs
    thr = thr_ref[slot]

    def step():
        for g in range(groups):
            key_sum = None
            for h in range(g * per, (g + 1) * per):
                s = dot(block[g], q_ref[h], 1, 1) * (scale * LOG2E)
                if not uniform:
                    s = masked(s, thr, causal)
                p = jnp.exp2(s - log_ref[h : h + 1, :])
                dp = dot(block[groups + g], grad_ref[h], 1, 1)
                ds = (p * (dp - delta_ref[h : h + 1, :])).astype(BF16)
                key_part = dot(ds, q_ref[h], 1, 0)
                value_part = dot(p.astype(BF16), grad_ref[h], 1, 0)
                query_part = dot(block[g], ds, 0, 0)
                if first:
                    dq_ref[h] = query_part
                else:
                    dq_ref[h] = dq_in[h] + query_part
                if key_sum is None:
                    key_sum, value_sum = key_part, value_part
                else:
                    key_sum, value_sum = key_sum + key_part, value_sum + value_part
            out_ref[g] = (key_sum * scale).astype(out_ref.dtype)
            out_ref[groups + g] = value_sum.astype(out_ref.dtype)

    if uniform:
        pl.when(thr == 0)(step)

        @pl.when(thr != 0)
        def _():
            out_ref[...] = jnp.zeros_like(out_ref)
            if first:
                dq_ref[...] = jnp.zeros_like(dq_ref)
            else:
                dq_ref[...] = dq_in[...]

    else:
        step()


def query_kernel(scale, dq_ref, out_ref):
    for h in range(dq_ref.shape[0]):
        out_ref[h] = (dq_ref[h].T * scale).astype(BF16)


def send_order(count):
    steps = [2**level for level in range(count.bit_length() - 1)]
    along_z = [d for d in (16, 8, 4) if d in steps]
    return along_z + [d for d in reversed(steps) if d not in along_z]


def per_device(queries, keys, values, norm_gain, out_grad, window_reach, partner_mask):
    _, rows, heads, size = queries.shape
    groups = keys.shape[2]
    scale = 1.0 / math.sqrt(size)
    count = lax.axis_size("seq")
    mine = lax.axis_index("seq")
    levels = len([level for level in range(1, 11) if 2 ** (level + 1) <= count])
    features = heads * lax.axis_size("head") * size

    by_head = lambda x: x[0].transpose(1, 0, 2)
    block0 = jnp.concatenate([by_head(keys), by_head(values)], axis=0)
    steps = [2**level for level in range(levels + 1)]
    order = send_order(count)
    arrived = {}
    for d in order:
        arrived[d] = rotated(block0, d)
    q = by_head(queries)
    og = by_head(out_grad)
    reach = jnp.where(mine >= 1, rows - window_reach[0, 0], rows)
    far = jnp.array(steps[1:], jnp.int32)
    shut = jnp.where((partner_mask[0, 0] == 1) & (mine >= far), 0, rows)
    thr = jnp.concatenate([reach[None], shut]).astype(jnp.int32)
    kind = {0: (0, True, False), 1: (0, False, False)}
    for slot, d in enumerate(steps[1:], 1):
        kind[d] = (slot, False, True)

    smem = pl.BlockSpec(memory_space=pltpu.SMEM)
    vmem = pl.BlockSpec(memory_space=pltpu.VMEM)
    shape = lambda dims, dtype: jax.ShapeDtypeStruct(dims, dtype)
    state = [
        shape((heads, rows), F32),
        shape((heads, rows), F32),
        shape((heads, size, rows), F32),
    ]
    cost = lambda: pl.CostEstimate(
        flops=0, transcendentals=0, bytes_accessed=0
    )

    def call(kernel, operands, outs, scratch=()):
        return pl.pallas_call(
            kernel,
            out_shape=outs,
            in_specs=[smem] + [vmem] * (len(operands) - 1)
            if operands[0].dtype == jnp.int32
            else [vmem] * len(operands),
            out_specs=[vmem] * len(outs),
            scratch_shapes=scratch,
            cost_estimate=cost(),
        )(*operands)

    m, l, acc, sg = call(
        functools.partial(forward_kernel, (kind[0],), scale, True, False),
        [thr, q, block0, og, norm_gain],
        state + [shape((heads, size, rows), F32)],
    )
    for d in order[:0:-1]:
        m, l, acc = call(
            functools.partial(forward_kernel, (kind[d],), scale, False, False),
            [thr, q, arrived[d], m, l, acc],
            state,
        )
    attn, log_total, stats = call(
        functools.partial(forward_kernel, (kind[order[0]],), scale, False, True),
        [thr, q, arrived[order[0]], m, l, acc, sg],
        [shape((heads, size, rows), BF16), shape((heads, rows), F32), shape((2, rows), F32)],
        [pltpu.VMEM(s.shape, s.dtype) for s in state],
    )
    other = lax.ppermute(stats, "head", [(0, 1), (1, 0)])
    grad, delta = call(
        functools.partial(gradient_kernel, features),
        [stats, other, attn, sg],
        [shape((heads, rows, size), BF16), shape((heads, rows), F32)],
    )
    dq = None
    back = {}
    for d in order + [0]:
        part, dq = call(
            functools.partial(backward_kernel, kind[d], scale, dq is None),
            [thr, q, block0 if d == 0 else arrived[d], grad, log_total, delta]
            + ([] if dq is None else [dq]),
            [
                shape((2 * groups, rows, size), F32 if d == 0 else BF16),
                shape((heads, size, rows), F32),
            ],
        )
        back[d] = part if d == 0 else rotated(part, -d)
    (normed,) = call(
        functools.partial(normed_kernel, features),
        [stats, other, attn, norm_gain],
        [shape((heads, rows, size), BF16)],
    )
    (query_grad,) = call(
        functools.partial(query_kernel, scale), [dq], [shape((heads, rows, size), BF16)]
    )
    total = back[0]
    for d in order:
        total = total + back[d].astype(F32)
    total = total.astype(BF16)
    by_token = lambda x: x.transpose(1, 0, 2)[None]
    return (
        by_token(normed),
        by_token(query_grad),
        by_token(total[:groups]),
        by_token(total[groups:]),
    )


def solution(mesh):
    spec = P(None, "seq", "head", None)
    return jax.shard_map(
        per_device,
        mesh=mesh,
        in_specs=(spec, spec, spec, P("head", None), spec, P(None, "seq"), P(None, "seq", None)),
        out_specs=(spec, spec, spec, spec),
        check_vma=False,
    )
```

```python
import functools
import math

import jax
import jax.numpy as jnp
from jax import lax
from jax.experimental import pallas as pl
from jax.experimental.pallas import tpu as pltpu
from jax.sharding import PartitionSpec as P


epsilon = 1e-06
NEG = -1e30
LOG2E = 1.4426950408889634
F32, BF16 = jnp.float32, jnp.bfloat16
onchip = pltpu.VMEM


def held(x):
    return pltpu.with_memory_space_constraint(x, pltpu.VMEM)


def rotated(value, steps):
    count = lax.axis_size("seq")
    return lax.ppermute(value, "seq", [(s, (s + steps) % count) for s in range(count)])


def dot(a, b, ca, cb):
    return lax.dot_general(a, b, (((ca,), (cb,)), ((), ())), preferred_element_type=F32)


def masked(scores, thr, causal, rows):
    keys = lax.broadcasted_iota(jnp.int32, scores.shape, 0)
    if causal:
        tokens = lax.rem(lax.broadcasted_iota(jnp.int32, scores.shape, 1), rows)
        return jnp.where(keys <= tokens, scores, NEG)
    return jnp.where(keys >= thr, scores, NEG)


def each_group(groups, body):
    def step(g, carry):
        body(g)
        return carry

    lax.fori_loop(0, groups, step, 0)


def forward_kernel(kind, scale, first, last, thr_ref, q_ref, block, *refs):
    slot, causal, uniform = kind
    groups, rows = q_ref.shape[0], block.shape[1]
    per = q_ref.shape[1] // rows
    thr = thr_ref[slot]
    if first:
        og_ref, gain_ref, m_ref, l_ref, acc_ref, sg_ref = refs
    elif last:
        m_in, l_in, acc_in, sg_ref, attn_ref, log_ref, stats_ref = refs
        stats_ref[...] = jnp.zeros_like(stats_ref)
    else:
        m_in, l_in, acc_in, m_ref, l_ref, acc_ref = refs

    def finish(g, m, l, acc):
        if not last:
            m_ref[g], l_ref[g], acc_ref[g] = m, l, acc
            return
        log_ref[g] = m + jnp.log2(l)
        attn = (acc * (1.0 / l)).astype(BF16)
        attn_ref[g] = attn
        wide = attn.astype(F32)
        square = jnp.sum(wide * wide, axis=0, keepdims=True)
        inner = jnp.sum(sg_ref[g] * wide, axis=0, keepdims=True)
        for i in range(per):
            cut = slice(i * rows, (i + 1) * rows)
            stats_ref[0:1, :] += square[:, cut]
            stats_ref[1:2, :] += inner[:, cut]

    def work(g):
        s = dot(block[g], q_ref[g], 1, 1) * (scale * LOG2E)
        if not uniform:
            s = masked(s, thr, causal, rows)
        m = jnp.max(s, axis=0, keepdims=True)
        if not first:
            m = jnp.maximum(m_in[g], m)
        p = jnp.exp2(s - m)
        l = jnp.sum(p, axis=0, keepdims=True)
        acc = dot(block[groups + g], p.astype(BF16), 0, 0)
        if not first:
            alpha = jnp.exp2(m_in[g] - m)
            l = l_in[g] * alpha + l
            acc = acc_in[g] * alpha + acc
        finish(g, m, l, acc)
        if first:
            for i in range(per):
                cut = slice(i * rows, (i + 1) * rows)
                wide = og_ref[g, cut, :].astype(F32) * gain_ref[pl.ds(g * per + i, 1), :]
                sg_ref[g, :, cut] = wide.T

    if uniform:
        pl.when(thr == 0)(lambda: each_group(groups, work))
        pl.when(thr != 0)(
            lambda: each_group(groups, lambda g: finish(g, m_in[g], l_in[g], acc_in[g]))
        )
    else:
        each_group(groups, work)


def gradient_kernel(features, mine_ref, other_ref, attn_ref, sg_ref, grad_ref, delta_ref):
    rows = mine_ref.shape[1]
    per = attn_ref.shape[2] // rows
    stats = mine_ref[...] + other_ref[...]
    inverse = lax.rsqrt(stats[0:1, :] / features + epsilon)
    back = stats[1:2, :] * (inverse * inverse * inverse) / features

    def work(g):
        for i in range(per):
            cut = slice(i * rows, (i + 1) * rows)
            wide = attn_ref[g, :, cut].astype(F32)
            grad = (sg_ref[g, :, cut] * inverse - wide * back).astype(BF16)
            delta_ref[g, :, cut] = jnp.sum(grad.astype(F32) * wide, axis=0, keepdims=True)
            grad_ref[g, cut, :] = grad.T

    each_group(attn_ref.shape[0], work)


def normed_kernel(features, mine_ref, other_ref, attn_ref, gain_ref, normed_ref):
    rows = mine_ref.shape[1]
    per = attn_ref.shape[2] // rows
    stats = mine_ref[0:1, :] + other_ref[0:1, :]
    inverse = lax.rsqrt(stats / features + epsilon)

    def work(g):
        for i in range(per):
            cut = slice(i * rows, (i + 1) * rows)
            wide = attn_ref[g, :, cut].astype(F32) * inverse
            normed_ref[g, cut, :] = (wide.T * gain_ref[pl.ds(g * per + i, 1), :]).astype(BF16)

    each_group(attn_ref.shape[0], work)


def backward_kernel(kind, scale, first, thr_ref, q_ref, block, grad_ref, log_ref, delta_ref, *refs):
    slot, causal, uniform = kind
    groups, rows = q_ref.shape[0], block.shape[1]
    if first:
        out_ref, dq_ref = refs
    else:
        dq_in, out_ref, dq_ref = refs
    thr = thr_ref[slot]

    def work(g):
        s = dot(block[g], q_ref[g], 1, 1) * (scale * LOG2E)
        if not uniform:
            s = masked(s, thr, causal, rows)
        p = jnp.exp2(s - log_ref[g])
        dp = dot(block[groups + g], grad_ref[g], 1, 1)
        ds = (p * (dp - delta_ref[g])).astype(BF16)
        out_ref[g] = (dot(ds, q_ref[g], 1, 0) * scale).astype(out_ref.dtype)
        out_ref[groups + g] = dot(p.astype(BF16), grad_ref[g], 1, 0).astype(out_ref.dtype)
        part = dot(block[g], ds, 0, 0)
        dq_ref[g] = part if first else dq_in[g] + part

    if uniform:
        pl.when(thr == 0)(lambda: each_group(groups, work))

        @pl.when(thr != 0)
        def _():
            out_ref[...] = jnp.zeros_like(out_ref)
            dq_ref[...] = jnp.zeros_like(dq_ref) if first else dq_in[...]

    else:
        each_group(groups, work)


def query_kernel(scale, rows, dq_ref, out_ref):
    def work(g):
        for i in range(dq_ref.shape[2] // rows):
            cut = slice(i * rows, (i + 1) * rows)
            out_ref[g, cut, :] = (dq_ref[g, :, cut].T * scale).astype(BF16)

    each_group(dq_ref.shape[0], work)


def send_order(count):
    steps = [2**level for level in range(count.bit_length() - 1)]
    along_z = [d for d in (16, 8, 4) if d in steps]
    return along_z + [d for d in reversed(steps) if d not in along_z]


def per_device(queries, keys, values, norm_gain, out_grad, window_reach, partner_mask):
    _, rows, heads, size = queries.shape
    groups = keys.shape[2]
    scale = 1.0 / math.sqrt(size)
    count = lax.axis_size("seq")
    mine = lax.axis_index("seq")
    levels = len([level for level in range(1, 11) if 2 ** (level + 1) <= count])
    features = heads * lax.axis_size("head") * size

    by_head = lambda x: x[0].transpose(1, 0, 2)
    block0 = jnp.concatenate([by_head(keys), by_head(values)], axis=0)
    steps = [2**level for level in range(levels + 1)]
    order = send_order(count)
    arrived = {}
    for d in order:
        arrived[d] = rotated(block0, d)
    wide = heads // groups * rows
    q = by_head(queries).reshape(groups, wide, size)
    og = by_head(out_grad).reshape(groups, wide, size)
    reach = jnp.where(mine >= 1, rows - window_reach[0, 0], rows)
    far = jnp.array(steps[1:], jnp.int32)
    shut = jnp.where((partner_mask[0, 0] == 1) & (mine >= far), 0, rows)
    thr = jnp.concatenate([reach[None], shut]).astype(jnp.int32)
    kind = {0: (0, True, False), 1: (0, False, False)}
    for slot, d in enumerate(steps[1:], 1):
        kind[d] = (slot, False, True)

    smem = pl.BlockSpec(memory_space=pltpu.SMEM)
    vmem = pl.BlockSpec(memory_space=pltpu.VMEM)
    row = (groups, 1, wide)
    tall = (groups, size, wide)
    state = [onchip(row, F32), onchip(row, F32), onchip(tall, F32)]

    def call(kernel, operands, outs, limit=16):
        return pl.pallas_call(
            kernel,
            out_shape=outs,
            in_specs=[smem if x.dtype == jnp.int32 else vmem for x in operands],
            out_specs=[vmem] * len(outs),
            compiler_params=pltpu.CompilerParams(vmem_limit_bytes=limit * 2**20),
            cost_estimate=pl.CostEstimate(flops=0, transcendentals=0, bytes_accessed=0),
        )(*[x if x.dtype == jnp.int32 else held(x) for x in operands])

    m, l, acc, sg = call(
        functools.partial(forward_kernel, kind[0], scale, True, False),
        [thr, q, block0, og, norm_gain],
        state + [onchip(tall, F32)],
    )
    for d in order[:0:-1]:
        m, l, acc = call(
            functools.partial(forward_kernel, kind[d], scale, False, False),
            [thr, q, arrived[d], m, l, acc],
            state,
        )
    attn, log_total, stats = call(
        functools.partial(forward_kernel, kind[order[0]], scale, False, True),
        [thr, q, arrived[order[0]], m, l, acc, sg],
        [onchip(tall, BF16), onchip(row, F32), onchip((2, rows), F32)],
    )
    other = lax.ppermute(stats, "head", [(0, 1), (1, 0)])
    grad, delta = call(
        functools.partial(gradient_kernel, features),
        [stats, other, attn, sg],
        [onchip((groups, wide, size), BF16), onchip(row, F32)],
    )
    dq = None
    back = {}
    for d in order + [0]:
        part, dq = call(
            functools.partial(backward_kernel, kind[d], scale, dq is None),
            [thr, q, block0 if d == 0 else arrived[d], grad, log_total, delta]
            + ([] if dq is None else [dq]),
            [
                onchip((2 * groups, rows, size), F32 if d == 0 else BF16),
                onchip(tall, F32),
            ],
        )
        back[d] = part if d == 0 else rotated(part, -d)
    (normed,) = call(
        functools.partial(normed_kernel, features),
        [stats, other, attn, norm_gain],
        [onchip((groups, wide, size), BF16)],
    )
    (query_grad,) = call(
        functools.partial(query_kernel, scale, rows), [dq], [onchip((groups, wide, size), BF16)]
    )
    total = back[0]
    for d in order:
        total = total + back[d].astype(F32)
    total = total.astype(BF16)
    by_token = lambda x: x.reshape(-1, rows, size).transpose(1, 0, 2)[None]
    return (
        by_token(normed),
        by_token(query_grad),
        by_token(total[:groups]),
        by_token(total[groups:]),
    )


def solution(mesh):
    spec = P(None, "seq", "head", None)
    return jax.shard_map(
        per_device,
        mesh=mesh,
        in_specs=(spec, spec, spec, P("head", None), spec, P(None, "seq"), P(None, "seq", None)),
        out_specs=(spec, spec, spec, spec),
        check_vma=False,
    )
```
